32 devices in a mesh: seq: 4 (over x, core), wshard: 8 (over z, y).
Axes of the slice: x: 2, y: 2, z: 4, core: 2. Of those that a mesh axis runs over, the one named last changes fastest.
Arguments:
- tokens: bfloat16 [8, 2048, 2048], P('wshard', 'seq'), may hold values from -6 to 6
- cotangent: bfloat16 [8, 2048, 2048], P('wshard', 'seq'), may hold values from -6 to 6
- order: int32 [8, 2048], P('wshard'), may hold values from 0 to 2047, each once within a row
- sequence_lengths: int32 [8, 2], P('wshard'), may hold values from 1024 to 1024, as said below
- adapter_per_sequence: int32 [8, 2], P('wshard'), may hold values from 0 to 7
- first_norm_scale: bfloat16 [2048], replicated, may hold values from 0.5 to 1.5
- first_norm_bias: bfloat16 [2048], replicated, may hold values from -1.75 to 1.75
- query_key_value_weight: bfloat16 [2048, 6144], P('wshard'), may hold values from -0.125 to 0.125
- query_key_value_bias: bfloat16 [6144], replicated, may hold values from -1.75 to 1.75
- attention_output_weight: bfloat16 [2048, 2048], P('wshard'), may hold values from -0.5 to 0.5
- second_norm_scale: bfloat16 [2048], replicated, may hold values from 0.5 to 1.5
- second_norm_bias: bfloat16 [2048], replicated, may hold values from -1.75 to 1.75
- gate_up_weight: bfloat16 [2048, 11264], P('wshard'), may hold values from -0.125 to 0.125
- down_weight: bfloat16 [5632, 2048], P('wshard'), may hold values from -0.078125 to 0.078125
- first_factors_width: bfloat16 [6, 2048, 128], replicated, may hold values from -0.125 to 0.125
- first_factors_hidden: bfloat16 [5632, 128], replicated, may hold values from -0.078125 to 0.078125
- second_factors_width: bfloat16 [5, 2048, 128], replicated, may hold values from -0.75 to 0.75
- second_factors_hidden: bfloat16 [2, 5632, 128], replicated, may hold values from -0.75 to 0.75
Outputs:
- mixed: bfloat16 [8, 2048, 2048], P('wshard', 'seq')
- grad_tokens: bfloat16 [8, 2048, 2048], P('wshard', 'seq')
- grad_lora_in_d: float32 [6, 2048, 128], P(None, None, ('seq', 'wshard'))
- grad_lora_in_ff: float32 [5632, 128], P(None, ('seq', 'wshard'))
- grad_lora_out_d: float32 [5, 2048, 128], P(None, None, ('seq', 'wshard'))
- grad_lora_out_ff: float32 [2, 5632, 128], P(None, None, ('seq', 'wshard'))
The draws below stay inside these ranges and needn't reach their ends.
Inputs may be any that keep to these rules, and one draw needn't show every extreme that they name: Each row of order is a permutation. `sequence_lengths`: each row sums to 2048; every length is at least 1024.
All inputs are finite; a program needn't handle non-finite values.
Results may differ from the reference program's by a relative error of at most 0.015.
Values may be sent and summed in bfloat16 or wider, within the bound.
No kernel may reach another device: no remote copies, remote signals or barrier semaphores. Data moves between devices by JAX's collectives and lax.ppermute only.
A program may use at most 384 MiB of HBM per device.

```python
import math
import jax
import jax.numpy as jnp
from jax import lax

MODEL_WIDTH = 2048
HEADS = 32
HEAD_DIM = 64
ROT = 16
HIDDEN_UNITS = 5632
ADAPTER_RANK = 16
ADAPTER_COUNT = 8
MINLEN = 1024
SEQS = 2
GROUPS = 8
GROUP_TOK = 2048


def draw_sequence_lengths(key, part):
    extra = GROUP_TOK - SEQS * MINLEN
    cut_key = jax.random.fold_in(key, 11)
    pick_key = jax.random.fold_in(key, 23)
    cuts = jnp.sort(jax.random.randint(cut_key, (GROUPS, SEQS - 1), 0, extra + 1), axis=1)
    bounds = jnp.concatenate([jnp.zeros((GROUPS, 1), jnp.int32), cuts.astype(jnp.int32), jnp.full((GROUPS, 1), extra, jnp.int32)], axis=1)
    pieces = bounds[:, 1:] - bounds[:, :-1]
    chosen = jax.random.randint(pick_key, (), 0, SEQS)
    first_row = (extra * (jnp.arange(SEQS) == chosen)).astype(jnp.int32)
    pieces = pieces.at[0].set(first_row)
    return (MINLEN + pieces).astype(jnp.int32)


def with_ends(drawn, stream_key, least, high):
    place = [jax.random.randint(jax.random.fold_in(stream_key, axis), (), 0, length) for axis, length in enumerate(drawn.shape)]
    widest = drawn.shape.index(max(drawn.shape))
    beside = place[:widest] + [(place[widest] + 1) % drawn.shape[widest]] + place[widest + 1:]
    return drawn.at[tuple(place)].set(least).at[tuple(beside)].set(high)


def block_levels(stream_key, shape, shards, low, top_value):
    gain = 1.0
    for axis_at, blocks in shards:
        steps = jax.random.uniform(jax.random.fold_in(jax.random.fold_in(stream_key, 6), axis_at), (blocks,), jnp.float32, low / len(shards), top_value / len(shards))
        gain = gain * jnp.repeat(jnp.exp(steps), shape[axis_at] // blocks).reshape((-1,) + (1,) * (len(shape) - 1 - axis_at))
    return gain


def noise(own_key, shape, scale, reach, split=(), kind=jnp.bfloat16):
    values = scale * jax.random.normal(own_key, shape, jnp.float32)
    if split:
        values = values * block_levels(own_key, shape, split, -0.22, 0.18)
    return jnp.clip(values, -reach, reach).astype(kind)


def setup_inputs(seed: int = 0) -> dict:
    keys = jax.random.split(jax.random.key(seed), 19)
    tokens = noise(keys[0], (GROUPS, GROUP_TOK, MODEL_WIDTH), 1.0, 6.0, ((0, 8), (1, 4)))
    cotangent = noise(keys[1], (GROUPS, GROUP_TOK, MODEL_WIDTH), 1.0, 6.0, ((0, 8), (1, 4)))
    order = jax.vmap(lambda own: jax.random.permutation(own, GROUP_TOK))(jax.random.split(keys[2], GROUPS)).reshape((GROUPS, GROUP_TOK)).astype(jnp.int32)
    sequence_lengths = draw_sequence_lengths(jax.random.fold_in(keys[18], 71), 0)
    adapter_per_sequence = with_ends(jax.random.randint(keys[4], (GROUPS, SEQS), 0, ADAPTER_COUNT), jax.random.fold_in(keys[4], 1), 0, ADAPTER_COUNT - 1).astype(jnp.int32)
    first_norm_scale = jnp.clip(1.0 + 0.1 * jax.random.normal(keys[5], (MODEL_WIDTH,), jnp.float32), 0.5, 1.5).astype(jnp.bfloat16)
    first_norm_bias = noise(keys[6], (MODEL_WIDTH,), 0.3, 1.75)
    query_key_value_weight = noise(keys[7], (MODEL_WIDTH, 3 * MODEL_WIDTH), MODEL_WIDTH ** -0.5, 0.125, ((0, 8),))
    query_key_value_bias = noise(keys[8], (3 * MODEL_WIDTH,), 0.3, 1.75)
    attention_output_weight = noise(keys[9], (MODEL_WIDTH, MODEL_WIDTH), (MODEL_WIDTH // 16) ** -0.5, 0.5, ((0, 8),))
    second_norm_scale = jnp.clip(1.0 + 0.1 * jax.random.normal(keys[10], (MODEL_WIDTH,), jnp.float32), 0.5, 1.5).astype(jnp.bfloat16)
    second_norm_bias = noise(keys[11], (MODEL_WIDTH,), 0.3, 1.75)
    gate_up_weight = noise(keys[12], (MODEL_WIDTH, 2 * HIDDEN_UNITS), MODEL_WIDTH ** -0.5, 0.125, ((0, 8),))
    down_weight = noise(keys[13], (HIDDEN_UNITS, MODEL_WIDTH), HIDDEN_UNITS ** -0.5, 0.078125, ((0, 8),))
    first_factors_width = noise(keys[14], (6, MODEL_WIDTH, ADAPTER_COUNT * ADAPTER_RANK), MODEL_WIDTH ** -0.5, 0.125)
    first_factors_hidden = noise(keys[15], (HIDDEN_UNITS, ADAPTER_COUNT * ADAPTER_RANK), HIDDEN_UNITS ** -0.5, 0.078125)
    second_factors_width = noise(keys[16], (5, MODEL_WIDTH, ADAPTER_COUNT * ADAPTER_RANK), (4 * ADAPTER_RANK) ** -0.5, 0.75)
    second_factors_hidden = noise(keys[17], (2, HIDDEN_UNITS, ADAPTER_COUNT * ADAPTER_RANK), (4 * ADAPTER_RANK) ** -0.5, 0.75)
    return dict(tokens=tokens, cotangent=cotangent, order=order, sequence_lengths=sequence_lengths, adapter_per_sequence=adapter_per_sequence, first_norm_scale=first_norm_scale, first_norm_bias=first_norm_bias, query_key_value_weight=query_key_value_weight, query_key_value_bias=query_key_value_bias, attention_output_weight=attention_output_weight, second_norm_scale=second_norm_scale, second_norm_bias=second_norm_bias, gate_up_weight=gate_up_weight, down_weight=down_weight, first_factors_width=first_factors_width, first_factors_hidden=first_factors_hidden, second_factors_width=second_factors_width, second_factors_hidden=second_factors_hidden)


NORM_EPS = 1e-05
NEG_FILL = -1e+30
ROPE_BASE = 10000.0
HIGHEST = lax.Precision.HIGHEST

@jax.custom_vjp
def low(v):
    return lax.optimization_barrier(v.astype(jnp.bfloat16)).astype(jnp.float32)

@jax.custom_vjp
def low_back(v):
    return v

def low_keep(v):
    return (low(v), None)

def low_pass(kept, grad):
    return (grad,)

def back_keep(v):
    return (v, None)

def back_low(kept, grad):
    return (low(grad),)
low.defvjp(low_keep, low_pass)
low_back.defvjp(back_keep, back_low)

def matrix_product(product_operand, weights):
    return jnp.dot(product_operand, weights, precision=HIGHEST)

def layer_norm(values, norm_gain, norm_shift):
    center = values - lax.optimization_barrier(jnp.mean(values, axis=-1, keepdims=True))
    spread = lax.optimization_barrier(jnp.mean(center * center, axis=-1, keepdims=True))
    return center * lax.rsqrt(spread + NORM_EPS) * norm_gain + norm_shift

def token_info(order_row, lengths, idents):
    seq_count = lengths.shape[0]
    seq_ends = jnp.cumsum(lengths).astype(jnp.int32)
    starts = (seq_ends - lengths).astype(jnp.int32)
    segment = lax.optimization_barrier(jnp.sum((order_row[:, None] >= seq_ends[None, :]).astype(jnp.int32), axis=1)).astype(jnp.int32)
    onehot = segment[:, None] == jnp.arange(seq_count, dtype=jnp.int32)[None, :]
    seg_begin = lax.optimization_barrier(jnp.sum(jnp.where(onehot, starts[None, :], 0), axis=1)).astype(jnp.int32)
    adapter = lax.optimization_barrier(jnp.sum(jnp.where(onehot, idents[None, :], 0), axis=1)).astype(jnp.int32)
    position = (order_row - seg_begin).astype(jnp.float32)
    columns = jnp.arange(ADAPTER_COUNT * ADAPTER_RANK, dtype=jnp.int32) // ADAPTER_RANK
    select_adapter = (columns[None, :] == adapter[:, None]).astype(jnp.float32)
    return (segment, position, select_adapter)

def rope_tables(position):
    half_rot = ROT // 2
    frequency = jnp.exp(jnp.arange(half_rot, dtype=jnp.float32) * (-2.0 * math.log(ROPE_BASE) / ROT))
    angles = position[:, None] * frequency[None, :]
    return (jnp.cos(angles), jnp.sin(angles))

def rotate(values, cosine, sine_tab):
    half_rot = ROT // 2
    first_half = values[..., :half_rot]
    second_half = values[..., half_rot:ROT]
    cos_wide = cosine[:, None, :]
    sin_wide = sine_tab[:, None, :]
    return jnp.concatenate([first_half * cos_wide - second_half * sin_wide, second_half * cos_wide + first_half * sin_wide, values[..., ROT:]], axis=-1)

def attention(q_rot, k_rot, v_all, segment, order_row):
    group_rows = q_rot.shape[0]
    qblock = min(512, group_rows)
    score_scale = 1.0 / math.sqrt(HEAD_DIM)

    def one_block(block_idx):
        row_start = block_idx * qblock
        rows_q = lax.dynamic_slice_in_dim(q_rot, row_start, qblock, 0)
        seg_q = lax.dynamic_slice_in_dim(segment, row_start, qblock, 0)
        ord_q = lax.dynamic_slice_in_dim(order_row, row_start, qblock, 0)
        scores = low_back(jnp.einsum('qhd,khd->hqk', rows_q, k_rot, precision=HIGHEST) * score_scale)
        allowed = (seg_q[:, None] == segment[None, :]) & (order_row[None, :] <= ord_q[:, None])
        scores = jnp.where(allowed[None], scores, NEG_FILL)
        row_max = lax.optimization_barrier(jnp.max(scores, axis=-1, keepdims=True))
        expo = jnp.exp(scores - row_max)
        probs = expo / lax.optimization_barrier(jnp.sum(expo, axis=-1, keepdims=True))
        return jnp.einsum('hqk,khd->qhd', low(probs), v_all, precision=HIGHEST)
    blocks = lax.map(jax.checkpoint(one_block), jnp.arange(group_rows // qblock, dtype=jnp.int32))
    return blocks.reshape(group_rows, q_rot.shape[1], q_rot.shape[2])

def adapter_delta(product_operand, low_rank_first, low_rank_second, select_adapter):
    inner_product = low(low_back(select_adapter * matrix_product(product_operand, low_rank_first)))
    return matrix_product(inner_product, low_rank_second.T)

def layer(input_rows, order_row, lengths, idents, in_d, in_ff, out_d, out_ff, frozen):
    first_norm_scale, first_norm_bias, query_key_value_weight, query_key_value_bias, attention_output_weight, second_norm_scale, second_norm_bias, gate_up_weight, down_weight = frozen
    segment, position, select_adapter = token_info(order_row, lengths, idents)
    row_count = input_rows.shape[0]
    heads_shape = (row_count, HEADS, HEAD_DIM)
    normed = low(layer_norm(input_rows, first_norm_scale, first_norm_bias))
    joint_qkv = matrix_product(normed, query_key_value_weight) + query_key_value_bias
    projected = []
    for projection_index in range(3):
        proj_value = joint_qkv[:, projection_index * MODEL_WIDTH:(projection_index + 1) * MODEL_WIDTH] + adapter_delta(normed, in_d[projection_index], out_d[projection_index], select_adapter)
        projected.append(low(low_back(proj_value)).reshape(heads_shape))
    cosine, sine_tab = rope_tables(position)
    q_rot = low(rotate(projected[0], cosine, sine_tab))
    k_rot = low(rotate(projected[1], cosine, sine_tab))
    attended = low(low_back(attention(q_rot, k_rot, projected[2], segment, order_row))).reshape(row_count, MODEL_WIDTH)
    residual_branch = low_back(matrix_product(attended, attention_output_weight) + adapter_delta(attended, in_d[3], out_d[3], select_adapter))
    incoming_hidden = input_rows + residual_branch
    normed_two = low(layer_norm(incoming_hidden, second_norm_scale, second_norm_bias))
    joint_gate_up = matrix_product(normed_two, gate_up_weight)
    gate_activation = low_back(joint_gate_up[:, :HIDDEN_UNITS] + adapter_delta(normed_two, in_d[4], out_ff[0], select_adapter))
    up_activation = low_back(joint_gate_up[:, HIDDEN_UNITS:] + adapter_delta(normed_two, in_d[5], out_ff[1], select_adapter))
    hidden_state = low(jax.nn.silu(gate_activation) * up_activation)
    residual_branch_second = low_back(matrix_product(hidden_state, down_weight) + adapter_delta(hidden_state, in_ff, out_d[4], select_adapter))
    return incoming_hidden + residual_branch_second

def reference(tokens, cotangent, order, sequence_lengths, adapter_per_sequence, first_norm_scale, first_norm_bias, query_key_value_weight, query_key_value_bias, attention_output_weight, second_norm_scale, second_norm_bias, gate_up_weight, down_weight, first_factors_width, first_factors_hidden, second_factors_width, second_factors_hidden):
    frozen = tuple((array_in.astype(jnp.float32) for array_in in (first_norm_scale, first_norm_bias, query_key_value_weight, query_key_value_bias, attention_output_weight, second_norm_scale, second_norm_bias, gate_up_weight, down_weight)))

    def layer_forward(x_all, in_d, in_ff, out_d, out_ff):

        def per_group(carry_in, group_data):
            input_rows, order_row, lengths, idents = group_data
            result = jax.checkpoint(layer)(input_rows, order_row, lengths, idents, in_d, in_ff, out_d, out_ff, frozen)
            return (carry_in, result)
        unused, mixed_output = lax.scan(per_group, jnp.zeros((), jnp.float32), (x_all, order, sequence_lengths, adapter_per_sequence))
        return mixed_output
    mixed_output, reverse_function = jax.vjp(layer_forward, tokens.astype(jnp.float32), first_factors_width.astype(jnp.float32), first_factors_hidden.astype(jnp.float32), second_factors_width.astype(jnp.float32), second_factors_hidden.astype(jnp.float32))
    grads = reverse_function(cotangent.astype(jnp.float32))
    return (mixed_output.astype(jnp.bfloat16), grads[0].astype(jnp.bfloat16), grads[1], grads[2], grads[3], grads[4])
```

```python
import math

import jax
import jax.numpy as jnp
from jax import lax
from jax.sharding import PartitionSpec as P

MODEL_WIDTH = 2048
HEAD_DIM = 64
ROT = 16
HIDDEN_UNITS = 5632
ADAPTER_RANK = 16
ADAPTER_COUNT = 8


NORM_EPS = 1e-05
NEG_FILL = -1e30
ROPE_BASE = 10000.0
CONTRACT_FINAL = (((1,), (1,)), ((), ()))
CONTRACT_FIRST = (((0,), (0,)), ((), ()))


def token_info(order_row, lengths, idents):
    seq_count = lengths.shape[0]
    seq_ends = jnp.cumsum(lengths)
    starts = seq_ends - lengths
    segment = jnp.sum((order_row[:, None] >= seq_ends[None, :]).astype(jnp.int32), axis=1)
    onehot = segment[:, None] == jnp.arange(seq_count, dtype=jnp.int32)[None, :]
    seg_begin = jnp.sum(jnp.where(onehot, starts[None, :], 0), axis=1)
    adapter = jnp.sum(jnp.where(onehot, idents[None, :], 0), axis=1)
    position = (order_row - seg_begin).astype(jnp.float32)
    columns = jnp.arange(ADAPTER_COUNT * ADAPTER_RANK, dtype=jnp.int32) // ADAPTER_RANK
    select_adapter = (columns[None, :] == adapter[:, None]).astype(jnp.float32)
    return (segment, position, select_adapter)


def rope_tables(position):
    half_rot = ROT // 2
    frequency = jnp.exp(
        jnp.arange(half_rot, dtype=jnp.float32) * (-2.0 * math.log(ROPE_BASE) / ROT)
    )
    angles = position[:, None] * frequency[None, :]
    return (jnp.cos(angles), jnp.sin(angles))


def rotate(values, cosine, sine_tab):
    half_rot = ROT // 2
    first_half = values[..., :half_rot]
    second_half = values[..., half_rot:ROT]
    cos_wide = cosine[:, None, :]
    sin_wide = sine_tab[:, None, :]
    return jnp.concatenate(
        [
            first_half * cos_wide - second_half * sin_wide,
            second_half * cos_wide + first_half * sin_wide,
            values[..., ROT:],
        ],
        axis=-1,
    )


def unrotate(grads, cosine, sine_tab):
    half_rot = ROT // 2
    first_half = grads[..., :half_rot]
    second_half = grads[..., half_rot:ROT]
    cos_wide = cosine[:, None, :]
    sin_wide = sine_tab[:, None, :]
    return jnp.concatenate(
        [
            first_half * cos_wide + second_half * sin_wide,
            second_half * cos_wide - first_half * sin_wide,
            grads[..., ROT:],
        ],
        axis=-1,
    )


def norm_forward(values, norm_gain, norm_shift):
    center = values - jnp.mean(values, axis=-1, keepdims=True)
    spread = jnp.mean(center * center, axis=-1, keepdims=True)
    inverse = lax.rsqrt(spread + NORM_EPS)
    scaled = center * inverse
    return (scaled * norm_gain + norm_shift, scaled, inverse)


def norm_backward(grad_in, scaled, inverse, norm_gain):
    dscaled = grad_in * norm_gain
    return inverse * (
        dscaled
        - jnp.mean(dscaled, axis=-1, keepdims=True)
        - scaled * jnp.mean(dscaled * scaled, axis=-1, keepdims=True)
    )


def low_rank_inner(product_operand, low_rank_first, select_adapter):
    return (
        select_adapter
        * jnp.dot(product_operand, low_rank_first, preferred_element_type=jnp.float32)
    ).astype(jnp.bfloat16)


def apply_low_rank(inner_product, low_rank_second):
    return lax.dot_general(
        inner_product, low_rank_second, CONTRACT_FINAL, preferred_element_type=jnp.float32
    )


def low_rank_backward(
    product_operand, row_gradients, inner_product, low_rank_first, low_rank_second, select_adapter
):
    output_factor_gradient = lax.dot_general(
        row_gradients, inner_product, CONTRACT_FIRST, preferred_element_type=jnp.float32
    )
    reverse_result = (
        select_adapter * jnp.dot(row_gradients, low_rank_second, preferred_element_type=jnp.float32)
    ).astype(jnp.bfloat16)
    input_factor_gradient = lax.dot_general(
        product_operand, reverse_result, CONTRACT_FIRST, preferred_element_type=jnp.float32
    )
    input_gradient = lax.dot_general(
        reverse_result, low_rank_first, CONTRACT_FINAL, preferred_element_type=jnp.float32
    )
    return (input_factor_gradient, output_factor_gradient, input_gradient)


def gather_rows(shard):
    parts = lax.axis_size("seq")
    rows = shard.shape[0] // parts
    own = lax.dynamic_slice_in_dim(shard, lax.axis_index("seq") * rows, rows, 0)
    return lax.all_gather(own, ("wshard", "seq"), axis=0, tiled=True)


def row_fold(product_operand, weight_rows):
    return jnp.dot(product_operand, weight_rows, preferred_element_type=jnp.float32)


def col_product(row_gradients, weight_rows):
    return lax.dot_general(
        row_gradients, weight_rows, CONTRACT_FINAL, preferred_element_type=jnp.float32
    )


def masked_scores(rows_q, k_rot, seg_q, ord_q, segment, order_row, score_scale):
    scores = (
        jnp.einsum("qhd,khd->hqk", rows_q, k_rot, preferred_element_type=jnp.float32) * score_scale
    )
    allowed = (seg_q[:, None] == segment[None, :]) & (order_row[None, :] <= ord_q[:, None])
    return jnp.where(allowed[None], scores, NEG_FILL)


def local(
    tokens,
    cotangent,
    order,
    sequence_lengths,
    adapter_per_sequence,
    first_norm_scale,
    first_norm_bias,
    query_key_value_weight,
    query_key_value_bias,
    attention_output_weight,
    second_norm_scale,
    second_norm_bias,
    gate_up_weight,
    down_weight,
    first_factors_width,
    first_factors_hidden,
    second_factors_width,
    second_factors_hidden,
):
    f32 = jnp.float32
    to_brainfloat = jnp.bfloat16
    rows_dev = tokens.shape[1]
    order_row = order[0]
    group_rows = order_row.shape[0]
    segment, position, select_all = token_info(
        order_row, sequence_lengths[0], adapter_per_sequence[0]
    )
    row_base = lax.axis_index("seq") * rows_dev
    select_adapter = lax.dynamic_slice_in_dim(select_all, row_base, rows_dev, 0)
    input_rows = tokens[0].astype(f32)
    gain_one = first_norm_scale.astype(f32)
    gain_two = second_norm_scale.astype(f32)
    normed, scaled_one, inverse_one = norm_forward(
        input_rows, gain_one, first_norm_bias.astype(f32)
    )
    normalized_brain = normed.astype(to_brainfloat)
    joint_qkv = row_fold(
        normalized_brain, gather_rows(query_key_value_weight)
    )
    joint_qkv = joint_qkv + query_key_value_bias.astype(f32)
    query_key_value_inner = [
        low_rank_inner(normalized_brain, first_factors_width[projection_index], select_adapter)
        for projection_index in range(3)
    ]
    proj_tok = [
        (
            joint_qkv[:, projection_index * MODEL_WIDTH : (projection_index + 1) * MODEL_WIDTH]
            + apply_low_rank(
                query_key_value_inner[projection_index], second_factors_width[projection_index]
            )
        ).astype(to_brainfloat)
        for projection_index in range(3)
    ]
    q_heads, k_heads, v_heads = (
        lax.all_to_all(proj_tok[0], "seq", split_axis=1, concat_axis=0, tiled=True),
        lax.all_to_all(proj_tok[1], "seq", split_axis=1, concat_axis=0, tiled=True),
        lax.all_to_all(proj_tok[2], "seq", split_axis=1, concat_axis=0, tiled=True),
    )
    head_count = q_heads.shape[1] // HEAD_DIM
    heads_shape = (group_rows, head_count, HEAD_DIM)
    cosine, sine_tab = rope_tables(position)
    q_rot = rotate(q_heads.reshape(heads_shape).astype(f32), cosine, sine_tab).astype(to_brainfloat)
    k_rot = rotate(k_heads.reshape(heads_shape).astype(f32), cosine, sine_tab).astype(to_brainfloat)
    v_all = v_heads.reshape(heads_shape)
    qblock = min(512, group_rows)
    block_count = group_rows // qblock
    score_scale = 1.0 / math.sqrt(HEAD_DIM)

    def attend(block_idx):
        row_start = block_idx * qblock
        rows_q = lax.dynamic_slice_in_dim(q_rot, row_start, qblock, 0)
        seg_q = lax.dynamic_slice_in_dim(segment, row_start, qblock, 0)
        ord_q = lax.dynamic_slice_in_dim(order_row, row_start, qblock, 0)
        scores = masked_scores(rows_q, k_rot, seg_q, ord_q, segment, order_row, score_scale)
        row_max = jnp.max(scores, axis=-1, keepdims=True)
        expo = jnp.exp(scores - row_max)
        row_total = jnp.sum(expo, axis=-1, keepdims=True)
        probs = expo / row_total
        block_out = jnp.einsum(
            "hqk,khd->qhd", probs.astype(to_brainfloat), v_all, preferred_element_type=f32
        )
        return (block_out, (row_max + jnp.log(row_total))[..., 0])

    attended, log_norms = lax.map(attend, jnp.arange(block_count, dtype=jnp.int32))
    attended = attended.reshape(group_rows, head_count * HEAD_DIM).astype(to_brainfloat)
    attention_tokens = lax.all_to_all(attended, "seq", split_axis=0, concat_axis=1, tiled=True)
    output_inner_rows = low_rank_inner(attention_tokens, first_factors_width[3], select_adapter)
    residual_branch = row_fold(
        attention_tokens, gather_rows(attention_output_weight)
    )
    incoming_hidden = (
        input_rows + residual_branch + apply_low_rank(output_inner_rows, second_factors_width[3])
    )
    normed_two, scaled_two, inverse_two = norm_forward(
        incoming_hidden, gain_two, second_norm_bias.astype(f32)
    )
    normalized_second_brain = normed_two.astype(to_brainfloat)
    joint_gate_up = row_fold(
        normalized_second_brain, gather_rows(gate_up_weight)
    )
    gate_inner_rows = low_rank_inner(
        normalized_second_brain, first_factors_width[4], select_adapter
    )
    up_inner_rows = low_rank_inner(normalized_second_brain, first_factors_width[5], select_adapter)
    gate_activation = joint_gate_up[:, :HIDDEN_UNITS] + apply_low_rank(
        gate_inner_rows, second_factors_hidden[0]
    )
    up_activation = joint_gate_up[:, HIDDEN_UNITS:] + apply_low_rank(
        up_inner_rows, second_factors_hidden[1]
    )
    sigmoid_gate = jax.nn.sigmoid(gate_activation)
    silu_gate = gate_activation * sigmoid_gate
    hidden_state = (silu_gate * up_activation).astype(to_brainfloat)
    down_inner_rows = low_rank_inner(hidden_state, first_factors_hidden, select_adapter)
    residual_branch_second = row_fold(
        hidden_state, gather_rows(down_weight)
    )
    mixed = (
        incoming_hidden
        + residual_branch_second
        + apply_low_rank(down_inner_rows, second_factors_width[4])
    ).astype(to_brainfloat)
    mixed_gradient = cotangent[0]
    grad_top = mixed_gradient.astype(f32)
    down_first_factor, down_second_factor, down_reverse = low_rank_backward(
        hidden_state,
        mixed_gradient,
        down_inner_rows,
        first_factors_hidden,
        second_factors_width[4],
        select_adapter,
    )
    d_hidden = col_product(
        mixed_gradient, gather_rows(down_weight)
    )
    d_hidden = d_hidden + down_reverse
    gate_gradient = (
        d_hidden * up_activation * (sigmoid_gate * (1.0 + gate_activation * (1.0 - sigmoid_gate)))
    ).astype(to_brainfloat)
    up_gradient = (d_hidden * silu_gate).astype(to_brainfloat)
    gate_first_factor, gate_second_factor, gate_reverse = low_rank_backward(
        normalized_second_brain,
        gate_gradient,
        gate_inner_rows,
        first_factors_width[4],
        second_factors_hidden[0],
        select_adapter,
    )
    up_first_factor, up_second_factor, up_reverse = low_rank_backward(
        normalized_second_brain,
        up_gradient,
        up_inner_rows,
        first_factors_width[5],
        second_factors_hidden[1],
        select_adapter,
    )
    grad_gu = jnp.concatenate([gate_gradient, up_gradient], axis=1)
    d_normed_two = col_product(
        grad_gu, gather_rows(gate_up_weight)
    )
    d_normed_two = d_normed_two + gate_reverse + up_reverse
    d_hidden_in = grad_top + norm_backward(d_normed_two, scaled_two, inverse_two, gain_two)
    branch_gradient = d_hidden_in.astype(to_brainfloat)
    output_first_factor, output_second_factor, output_reverse = low_rank_backward(
        attention_tokens,
        branch_gradient,
        output_inner_rows,
        first_factors_width[3],
        second_factors_width[3],
        select_adapter,
    )
    d_att = col_product(
        branch_gradient, gather_rows(attention_output_weight)
    )
    d_att = (d_att + output_reverse).astype(to_brainfloat)
    d_heads = lax.all_to_all(d_att, "seq", split_axis=1, concat_axis=0, tiled=True).reshape(
        heads_shape
    )

    def attend_back(carry_in, block_idx):
        key_acc, value_acc = carry_in
        row_start = block_idx * qblock
        rows_q = lax.dynamic_slice_in_dim(q_rot, row_start, qblock, 0)
        seg_q = lax.dynamic_slice_in_dim(segment, row_start, qblock, 0)
        ord_q = lax.dynamic_slice_in_dim(order_row, row_start, qblock, 0)
        grad_q = lax.dynamic_slice_in_dim(d_heads, row_start, qblock, 0)
        scores = masked_scores(rows_q, k_rot, seg_q, ord_q, segment, order_row, score_scale)
        probs = jnp.exp(scores - log_norms[block_idx][..., None])
        value_acc = value_acc + jnp.einsum(
            "hqk,qhd->khd", probs.astype(to_brainfloat), grad_q, preferred_element_type=f32
        )
        d_probs = jnp.einsum("qhd,khd->hqk", grad_q, v_all, preferred_element_type=f32)
        d_scores = (probs * (d_probs - jnp.sum(probs * d_probs, axis=-1, keepdims=True))).astype(
            to_brainfloat
        )
        query_grad = (
            jnp.einsum("hqk,khd->qhd", d_scores, k_rot, preferred_element_type=f32) * score_scale
        )
        key_acc = (
            key_acc
            + jnp.einsum("hqk,qhd->khd", d_scores, rows_q, preferred_element_type=f32) * score_scale
        )
        return ((key_acc, value_acc), query_grad)

    zero_heads = jnp.zeros(heads_shape, f32)
    (key_grad, value_grad), query_grads = lax.scan(
        attend_back, (zero_heads, zero_heads), jnp.arange(block_count, dtype=jnp.int32)
    )
    flat_width = head_count * HEAD_DIM
    grad_q_heads = (
        unrotate(query_grads.reshape(heads_shape), cosine, sine_tab)
        .reshape(group_rows, flat_width)
        .astype(to_brainfloat)
    )
    grad_k_heads = (
        unrotate(key_grad, cosine, sine_tab).reshape(group_rows, flat_width).astype(to_brainfloat)
    )
    grad_v_heads = value_grad.reshape(group_rows, flat_width).astype(to_brainfloat)
    tok_q, tok_k, tok_v = (
        lax.all_to_all(grad_q_heads, "seq", split_axis=0, concat_axis=1, tiled=True),
        lax.all_to_all(grad_k_heads, "seq", split_axis=0, concat_axis=1, tiled=True),
        lax.all_to_all(grad_v_heads, "seq", split_axis=0, concat_axis=1, tiled=True),
    )
    grads_tok = [tok_q, tok_k, tok_v]
    in_qkv = []
    out_qkv = []
    back_sum = jnp.zeros((rows_dev, MODEL_WIDTH), f32)
    for projection_index in range(3):
        input_factor_gradient, output_factor_gradient, input_gradient = low_rank_backward(
            normalized_brain,
            grads_tok[projection_index],
            query_key_value_inner[projection_index],
            first_factors_width[projection_index],
            second_factors_width[projection_index],
            select_adapter,
        )
        in_qkv.append(input_factor_gradient)
        out_qkv.append(output_factor_gradient)
        back_sum = back_sum + input_gradient
    grad_qkv = jnp.concatenate(grads_tok, axis=1)
    d_normed = col_product(
        grad_qkv, gather_rows(query_key_value_weight)
    )
    d_normed = d_normed + back_sum
    grad_tokens = (d_hidden_in + norm_backward(d_normed, scaled_one, inverse_one, gain_one)).astype(
        to_brainfloat
    )
    stacked_in_d = jnp.stack(
        [in_qkv[0], in_qkv[1], in_qkv[2], output_first_factor, gate_first_factor, up_first_factor]
    )
    stacked_out_d = jnp.stack(
        [out_qkv[0], out_qkv[1], out_qkv[2], output_second_factor, down_second_factor]
    )
    stacked_out_ff = jnp.stack([gate_second_factor, up_second_factor])
    sum_in_d, sum_in_ff, sum_out_d, sum_out_ff = (
        lax.psum_scatter(stacked_in_d, ("seq", "wshard"), scatter_dimension=2, tiled=True),
        lax.psum_scatter(down_first_factor, ("seq", "wshard"), scatter_dimension=1, tiled=True),
        lax.psum_scatter(stacked_out_d, ("seq", "wshard"), scatter_dimension=2, tiled=True),
        lax.psum_scatter(stacked_out_ff, ("seq", "wshard"), scatter_dimension=2, tiled=True),
    )
    return (mixed[None], grad_tokens[None], sum_in_d, sum_in_ff, sum_out_d, sum_out_ff)


def solution(mesh):
    in_specs = (
        P("wshard", "seq", None),
        P("wshard", "seq", None),
        P("wshard", None),
        P("wshard", None),
        P("wshard", None),
        P(),
        P(),
        P("wshard", None),
        P(),
        P("wshard", None),
        P(),
        P(),
        P("wshard", None),
        P("wshard", None),
        P(),
        P(),
        P(),
        P(),
    )
    out_specs = (
        P("wshard", "seq", None),
        P("wshard", "seq", None),
        P(None, None, ("seq", "wshard")),
        P(None, ("seq", "wshard")),
        P(None, None, ("seq", "wshard")),
        P(None, None, ("seq", "wshard")),
    )
    return jax.shard_map(local, mesh=mesh, in_specs=in_specs, out_specs=out_specs, check_vma=False)
```
